512 devices in a mesh: wide: 64 (over x, y, z_hi), lane: 8 (over z_lo, core).
Axes of the slice: x: 4, y: 8, z: 8 (z_hi: 2, z_lo: 4; z = z_hi * 4 + z_lo), core: 2. Of those that a mesh axis runs over, the one named last changes fastest.
Arguments:
- source: float32 [131072, 256], P(('wide', 'lane')), may hold values from -80 to 80
- target: float32 [65536, 256], P(('wide', 'lane')), may hold values from -80 to 80
- observed: float32 [2, 131072, 128], P(None, ('wide', 'lane')), may hold values from -15 to 15
- tiles: int32 [2, 1024, 1], P(None, ('wide', 'lane')), may hold values 0 or 1
Outputs:
- new_source: float32 [131072, 256], P(('wide', 'lane'))
- carried_target: float32 [65536, 256], P(('wide', 'lane'))
The draws below stay inside these ranges and needn't reach their ends.
All inputs are finite; a program needn't handle non-finite values. No bound on the sum of `tiles` on one device may be relied on, other than what follows from the above.
Results may differ from the reference program's by a relative error of at most 0.00026.
Values sent between devices are 32-bit elements; how exact they have to be, the bound alone decides.
No kernel may reach another device: no remote copies, remote signals or barrier semaphores. Data moves between devices by JAX's collectives and lax.ppermute only.
A program may use at most 64 MiB of HBM per device.

```python
import math
import jax
import jax.numpy as jnp
from jax import lax

RANK = 256
SRC_DEV = 256
TGT_BLOCK = 128
VISITS = 2
TILE = 128
SRC_ROWS = 131072
TGT_ROWS = 65536
N_WIDE = 64
N_LANE = 8


def factor_draw(key, total_rows):
    key_columns, key_rows, key_entries = jax.random.split(key, 3)
    columns = jnp.exp(jax.random.uniform(key_columns, (RANK,), jnp.float32, math.log(0.4), math.log(2.5)))
    position = jnp.arange(total_rows, dtype=jnp.float32)[:, None] / total_rows
    entries = jnp.clip(jax.random.normal(key_entries, (total_rows, RANK), jnp.float32), -5.0, 5.0)
    spread = jnp.exp(jax.random.uniform(key_rows, (total_rows, 1), jnp.float32, math.log(0.7), math.log(1.4)))
    scales = jnp.exp(position * math.log(3.0)) * spread
    return 0.35 * entries * columns[None, :] * scales


def draw_source(key, part):
    return factor_draw(jax.random.fold_in(key, 11), SRC_ROWS)


def draw_target(key, part):
    return factor_draw(jax.random.fold_in(key, 23), TGT_ROWS)


def touch_ends(drawn, stream_key, low, largest):
    dims = drawn.shape
    place = [jax.random.randint(jax.random.fold_in(stream_key, axis), (), 0, dims[axis]) for axis in range(len(dims))]
    drawn = drawn.at[tuple(place)].set(low)
    longest = dims.index(max(dims))
    place[longest] = (place[longest] + 1) % dims[longest]
    return drawn.at[tuple(place)].set(largest)


def steps_of(key, shape, shards, least, high):
    level, own = 1.0, jax.random.fold_in(key, 6)
    for dim, blocks in shards:
        draws = jnp.exp(jax.random.uniform(jax.random.fold_in(own, dim), (blocks,), jnp.float32, least / len(shards), high / len(shards)))
        level = level * jnp.repeat(draws, shape[dim] // blocks).reshape([-1 if axis == dim else 1 for axis in range(len(shape))])
    return level


def gaussian(key, extent, scale, bound, cuts=(), held_as=jnp.bfloat16):
    values = jax.random.normal(key, extent, jnp.float32) * scale
    if len(cuts) > 0:
        values = steps_of(key, extent, cuts, -0.22, 0.18) * values
    return jnp.clip(values, min=-bound, max=bound).astype(held_as)


def setup_inputs(seed: int = 0) -> dict:
    keys = jax.random.split(jax.random.key(seed), 5)
    source = draw_source(jax.random.fold_in(keys[4], 71), 0)
    target = draw_target(jax.random.fold_in(keys[4], 71), 0)
    observed = gaussian(keys[2], (VISITS, SRC_ROWS, TGT_BLOCK), 3.0, 15.0, ((1, 512),), jnp.float32)
    tiles = touch_ends((jax.random.randint(keys[3], (VISITS, SRC_ROWS // TILE, TGT_BLOCK // TILE), 0, 2) < 1).astype(jnp.int32), jax.random.fold_in(keys[3], 1), 0, 1)
    return {"source": source, "target": target, "observed": observed, "tiles": tiles}


step_size = 0.0002

def precondition(gradient, factor):
    partial_value = lax.linalg.triangular_solve(factor, gradient, left_side=False, lower=True, transpose_a=True)
    return lax.linalg.triangular_solve(factor, partial_value, left_side=False, lower=True)

def reference(source, target, observed, tiles):
    highest = lax.Precision.HIGHEST
    source_blocks = source.reshape(N_WIDE, N_LANE, SRC_DEV, RANK)
    target_blocks = target.reshape(N_WIDE, N_LANE, TGT_BLOCK, RANK)
    observed_blocks = observed.reshape(VISITS, N_WIDE, N_LANE, SRC_DEV, TGT_BLOCK)
    tile_blocks = tiles.reshape(VISITS, N_WIDE, N_LANE, SRC_DEV // TILE, TGT_BLOCK // TILE)
    for visit_number in range(VISITS):
        gram_source = jnp.einsum('abir,abis->rs', source_blocks, source_blocks, precision=highest) / SRC_ROWS
        gram_target = jnp.einsum('abir,abis->rs', target_blocks, target_blocks, precision=highest) / TGT_ROWS
        factor_source = jnp.linalg.cholesky(gram_source)
        factor_target = jnp.linalg.cholesky(gram_target)
        expanded = jnp.repeat(jnp.repeat(tile_blocks[visit_number].astype(jnp.float32), TILE, axis=2), TILE, axis=3)
        predicted = jnp.einsum('abir,abjr->abij', source_blocks, target_blocks, precision=highest)
        residual = expanded * (predicted - observed_blocks[visit_number])
        grad_source = jnp.einsum('abij,abjr->abir', residual, target_blocks, precision=highest)
        grad_target = jnp.einsum('abij,abir->abjr', residual, source_blocks, precision=highest)
        step_source = precondition(grad_source.reshape(SRC_ROWS, RANK), factor_target)
        step_target = precondition(grad_target.reshape(TGT_ROWS, RANK), factor_source)
        source_blocks = source_blocks - step_size * step_source.reshape(source_blocks.shape)
        target_blocks = target_blocks - step_size * step_target.reshape(target_blocks.shape)
        target_blocks = jnp.roll(target_blocks, 1, axis=0)
    return (source_blocks.reshape(SRC_ROWS, RANK), target_blocks.reshape(TGT_ROWS, RANK))
```

```python
import jax
import jax.numpy as jnp
from jax import lax
from jax.experimental import pallas as pl
from jax.experimental.pallas import tpu as pltpu
from jax.sharding import Mesh
from jax.sharding import PartitionSpec as P

step_size = 0.0002

AXES = ("xh", "xl", "ya", "yb", "yc", "zh", "zla", "zlb", "core")
WIDE = ("xh", "xl", "ya", "yb", "yc", "zh")
SCATTER = ("xh", "xl", "yc", "zlb", "core")
EXCHANGE = ("ya", "yb", "zh", "zla")
PIECES = 32
BLOCK = 32


def product(left, right, left_dim, right_dim):
    return lax.dot_general(
        left,
        right,
        (((left_dim,), (right_dim,)), ((), ())),
        precision=lax.Precision.HIGHEST,
        preferred_element_type=jnp.float32,
    )


def grid_of(shape):
    return lax.broadcasted_iota(jnp.int32, shape, 0), lax.broadcasted_iota(jnp.int32, shape, 1)


def sweep_panel(panel, first):
    rows, cols = panel.shape
    sub, lane = grid_of((8, cols))
    one_lane = lax.broadcasted_iota(jnp.int32, (1, cols), 1)
    groups = [panel[8 * g : 8 * g + 8] for g in range(rows // 8)]
    for row in range(rows):
        pivot, own = first + row, row // 8
        columns = [jnp.broadcast_to(g[:, pivot : pivot + 1], (8, cols)) for g in groups]
        scale = 1.0 / columns[own][row % 8 : row % 8 + 1]
        line = groups[own][row % 8 : row % 8 + 1]
        line = jnp.where(one_lane == pivot, scale, line * scale)
        full = jnp.broadcast_to(line, (8, cols))
        swept = []
        for g in range(rows // 8):
            value = jnp.where(lane == pivot, 0.0, groups[g]) - columns[g] * full
            swept.append(jnp.where(sub == row % 8, full, value) if g == own else value)
        groups = swept
    return jnp.concatenate(groups, 0)


def invert_pair(ref):
    size = ref.shape[1]
    half = size // 2

    def one_half(_, carry):
        lane = lax.broadcasted_iota(jnp.int32, (size, size), 1)
        for block in range(half // BLOCK):
            start = block * BLOCK
            for t in range(2):
                ref[t, start : start + BLOCK, :] = sweep_panel(ref[t, start : start + BLOCK, :], start)
            inside = (lane >= start) & (lane < start + BLOCK)
            for t in range(2):
                panel = ref[t, start : start + BLOCK, :]
                whole = ref[t]
                ref[t] = jnp.where(inside, 0.0, whole) - product(whole[:, start : start + BLOCK], panel, 1, 0)
                ref[t, start : start + BLOCK, :] = panel
        for t in range(2):
            whole = ref[t]
            ref[t, :half, :half] = whole[half:, half:]
            ref[t, :half, half:] = whole[half:, :half]
            ref[t, half:, :half] = whole[:half, half:]
            ref[t, half:, half:] = whole[:half, :half]
        return carry

    lax.fori_loop(0, 2, one_half, 0)


def gradients(source, target, observed, upper, lower):
    row = lax.broadcasted_iota(jnp.int32, observed.shape, 0)
    mask = jnp.where(row < observed.shape[0] // 2, upper, lower).astype(jnp.float32)
    residual = mask * (product(source, target, 1, 1) - observed)
    return product(residual, target, 1, 0), product(residual, source, 0, 0)


def diagonal(square):
    row, col = grid_of(square.shape)
    return jnp.sum(jnp.where(row == col, square, 0.0), axis=0, keepdims=True)


def first_kernel(tiles, source_ref, target_ref, observed_ref, grad_ref, moving_ref, sums_ref):
    source, target = source_ref[...], target_ref[...]
    count = target.shape[0]
    grad_source, grad_target = gradients(source, target, observed_ref[0], tiles[0, 0], tiles[0, 1])
    grad_ref[...] = grad_source
    moving_ref[:count, :] = target
    moving_ref[count:, :] = grad_target
    gram_source = product(source, source, 0, 0)
    gram_target = product(target, target, 0, 0)
    cross = product(source, grad_source, 0, 0)
    square_source = product(grad_source, grad_source, 0, 0)
    square_target = product(grad_target, grad_target, 0, 0)
    row, col = grid_of(cross.shape)
    upper = row <= col
    packed = (
        cross,
        jnp.where(upper, gram_source, gram_target),
        jnp.where(upper, square_source, square_target),
    )
    for place, square in enumerate(packed):
        for side in range(2):
            rows = slice(16 * place + 8 * side, 16 * place + 8 * side + 8)
            sums_ref[:, rows, :] = square[:, 128 * side : 128 * side + 128].reshape(PIECES, 8, 128)
    sums_ref[:, 48:56, :] = jnp.zeros((PIECES, 8, 128), jnp.float32)
    for place, square in enumerate((gram_target, square_target)):
        line = diagonal(square)
        for side in range(2):
            slot = 48 + 2 * place + side
            sums_ref[0, slot : slot + 1, :] = line[:, 128 * side : 128 * side + 128]


def unpacked(sums_ref, place):
    halves = [sums_ref[:, 16 * place + 8 * side : 16 * place + 8 * side + 8, :].reshape(256, 128) for side in range(2)]
    return jnp.concatenate(halves, 1)


def unpacked_pair(sums_ref, place):
    packed = unpacked(sums_ref, place)
    flipped = packed.T
    row, col = grid_of(packed.shape)
    line = jnp.concatenate([sums_ref[0, 46 + 2 * place + side : 47 + 2 * place + side, :] for side in range(2)], 1)
    first = jnp.where(row <= col, packed, flipped)
    second = jnp.where(row > col, packed, flipped)
    return first, jnp.where(row == col, line, second)


def updated_gram(gram, cross, square, inverse):
    moved = product(cross, inverse, 1, 0)
    twice = product(product(inverse, square, 1, 0), inverse, 1, 0)
    return gram - step_size * (moved + moved.T) + (step_size * step_size) * twice


def second_kernel(
    source_rows, target_rows,
    tiles, sums_ref, source_ref, grad_ref, moving_ref, observed_ref,
    source_out, grad_out, moving_out, gram_out, work,
):
    count = moving_ref.shape[0] // 2
    gram_source, gram_target = unpacked_pair(sums_ref, 1)
    work[0] = gram_source / source_rows
    work[1] = gram_target / target_rows
    invert_pair(work)
    source = source_ref[...] - step_size * product(grad_ref[...], work[1], 1, 0)
    target = moving_ref[:count, :] - step_size * product(moving_ref[count:, :], work[0], 1, 0)
    source_out[...] = source
    moving_out[:count, :] = target
    grad_source, grad_target = gradients(source, target, observed_ref[1], tiles[1, 0], tiles[1, 1])
    grad_out[...] = grad_source
    moving_out[count:, :] = grad_target
    gram_source, gram_target = unpacked_pair(sums_ref, 1)
    square_source, square_target = unpacked_pair(sums_ref, 2)
    cross = unpacked(sums_ref, 0)
    gram_out[0] = updated_gram(gram_source, cross, square_source, work[1]) / source_rows
    gram_out[1] = updated_gram(gram_target, cross.T, square_target, work[0]) / target_rows


def third_kernel(gram_ref, source_ref, grad_ref, source_out, inverse_out, work):
    work[...] = gram_ref[...]
    invert_pair(work)
    source_out[...] = source_ref[...] - step_size * product(grad_ref[...], work[1], 1, 0)
    inverse_out[...] = work[0]


def last_kernel(moving_ref, inverse_ref, target_out):
    count = moving_ref.shape[0] // 2
    target_out[...] = moving_ref[:count, :] - step_size * product(moving_ref[count:, :], inverse_ref[...], 1, 0)


def call(kernel, shapes, scratch, *arguments, scalars=0):
    vmem = pl.BlockSpec(memory_space=pltpu.VMEM)
    smem = pl.BlockSpec(memory_space=pltpu.SMEM)
    return pl.pallas_call(
        kernel,
        out_shape=[jax.ShapeDtypeStruct(shape, jnp.float32) for shape in shapes],
        in_specs=[smem] * scalars + [vmem] * (len(arguments) - scalars),
        out_specs=[vmem] * len(shapes),
        scratch_shapes=[pltpu.VMEM(shape, jnp.float32) for shape in scratch],
    )(*arguments)


def next_position(value):
    count = lax.axis_size(WIDE)
    return lax.ppermute(value, WIDE, [(place, (place + 1) % count) for place in range(count)])


def exchanged(value, axes):
    return lax.all_to_all(value, axes, 0, 0, tiled=True)


def spread(value, axes):
    return exchanged(jnp.broadcast_to(value[None], (lax.axis_size(axes), *value.shape)), axes)


def on_device(source, target, observed, tiles):
    devices = lax.axis_size(AXES)
    source_rows = source.shape[0] * devices
    target_rows = target.shape[0] * devices
    flags = tiles.reshape(2, 2)
    square = (256, 256)
    grad, moving, sums = call(
        first_kernel, (square, square, (PIECES, 56, 128)), (), flags, source, target, observed, scalars=1
    )
    moving = next_position(moving)
    sums = jnp.sum(exchanged(sums, SCATTER), axis=0)
    sums = jnp.sum(spread(sums, EXCHANGE), axis=0)
    sums = spread(sums, SCATTER)

    def middle(*refs):
        second_kernel(source_rows, target_rows, *refs)

    source, grad, moving, grams = call(
        middle, (square, square, square, (2, *square)), ((2, *square),),
        flags, sums, source, grad, moving, observed, scalars=1,
    )
    moving = next_position(moving)
    source, inverse = call(third_kernel, (square, square), ((2, *square),), grams, source, grad)
    (target,) = call(last_kernel, (target.shape,), (), moving, inverse)
    return source, target


def solution(mesh):
    fine = Mesh(mesh.devices.reshape((2,) * len(AXES)), AXES)
    placed = (P(AXES, None), P(AXES, None), P(None, AXES, None), P(None, AXES, None))
    return jax.shard_map(
        on_device, mesh=fine, in_specs=placed, out_specs=(P(AXES, None), P(AXES, None)), check_vma=False
    )
```

```python
import jax
import jax.numpy as jnp
from jax import lax
from jax.experimental import pallas as pl
from jax.experimental.pallas import tpu as pltpu
from jax.sharding import Mesh
from jax.sharding import PartitionSpec as P

step_size = 0.0002

AXES = ("xh", "xl", "ya", "yb", "yc", "zh", "zla", "zlb", "core")
WIDE = ("xh", "xl", "ya", "yb", "yc", "zh")
SCATTER = ("xh", "xl", "yc", "zlb", "core")
EXCHANGE = ("ya", "yb", "zh", "zla")
PIECES = 32
BLOCK = 64


def product(left, right, left_dim, right_dim):
    return lax.dot_general(
        left,
        right,
        (((left_dim,), (right_dim,)), ((), ())),
        precision=lax.Precision.HIGHEST,
        preferred_element_type=jnp.float32,
    )


def grid_of(shape):
    return lax.broadcasted_iota(jnp.int32, shape, 0), lax.broadcasted_iota(jnp.int32, shape, 1)


def sweep_pair(panels, first):
    rows, cols = panels[0].shape
    sub, lane = grid_of((8, cols))
    if first:
        panels = [pltpu.roll(panel, cols - first, 1) for panel in panels]
    start = tuple(tuple(panel[8 * g : 8 * g + 8] for g in range(rows // 8)) for panel in panels)

    def wide(value):
        return jnp.broadcast_to(value, (8, cols))

    def eight_pivots(_, carry):
        held = [list(groups) for groups in carry]
        for r in range(0, 8, 2):
            here, after = lane == r, lane == r + 1
            for t, groups in enumerate(held):
                left = [wide(group[:, r : r + 1]) for group in groups]
                right = [wide(group[:, r + 1 : r + 2]) for group in groups]
                upper = jnp.where(after, 0.0, jnp.where(here, 1.0, wide(groups[0][r : r + 1])))
                lower = jnp.where(here, 0.0, jnp.where(after, 1.0, wide(groups[0][r + 1 : r + 2])))
                main = jnp.where(sub == r, left[0], right[0])
                cross = wide(jnp.where(sub == r, right[0], left[0])[r : r + 1])
                first_pivot, second_pivot = wide(main[r : r + 1]), wide(main[r + 1 : r + 2])
                scale = 1.0 / (first_pivot * second_pivot - cross * cross)
                upper, lower = (
                    scale * (second_pivot * upper - cross * lower),
                    scale * (first_pivot * lower - cross * upper),
                )
                swept = [
                    jnp.where(here | after, 0.0, group) - left[g] * upper - right[g] * lower
                    for g, group in enumerate(groups)
                ]
                swept[0] = jnp.where(sub == r, upper, jnp.where(sub == r + 1, lower, swept[0]))
                held[t] = swept
        return tuple(tuple(pltpu.roll(group, cols - 8, 1) for group in groups[1:] + groups[:1]) for groups in held)

    swept = [jnp.concatenate(groups, 0) for groups in lax.fori_loop(0, rows // 8, eight_pivots, start)]
    back = (first + rows) % cols
    return [pltpu.roll(panel, back, 1) for panel in swept] if back else swept


def invert_blocks(squares):
    size = squares[0].shape[0]
    lane = lax.broadcasted_iota(jnp.int32, (BLOCK, size), 1)
    panels = [[square[start : start + BLOCK] for start in range(0, size, BLOCK)] for square in squares]
    for block in range(size // BLOCK):
        start = block * BLOCK
        swept = sweep_pair([held[block] for held in panels], start)
        inside = (lane >= start) & (lane < start + BLOCK)
        for held, panel in zip(panels, swept):
            for other in range(len(held)):
                left = held[other][:, start : start + BLOCK]
                if other != block:
                    held[other] = jnp.where(inside, 0.0, held[other]) - product(left, panel, 1, 0)
            held[block] = panel
    return [jnp.concatenate(held, 0) for held in panels]


def invert_pair(ref):
    size = ref.shape[1]
    half = size // 2
    row, col = grid_of((size, size))
    scales = []
    for t in range(2):
        whole = ref[t]
        main = jnp.where(row == col, whole, 0.0)
        across = lax.rsqrt(jnp.sum(main, axis=0, keepdims=True))
        down = lax.rsqrt(jnp.sum(main, axis=1, keepdims=True))
        scales.append((across, down))
        ref[t] = whole * across * down
    leading = invert_blocks([ref[t, :half, :half] for t in range(2)])
    ratio = [product(leading[t], ref[t, :half, half:], 1, 0) for t in range(2)]
    rest = [ref[t, half:, half:] - product(ref[t, :half, half:], ratio[t], 0, 0) for t in range(2)]
    for t in range(2):
        ref[t, :half, :half] = leading[t]
        ref[t, :half, half:] = ratio[t]
    trailing = invert_blocks(rest)
    for t in range(2):
        across, down = scales[t]
        ratio = ref[t, :half, half:]
        corner = -product(ratio, trailing[t], 1, 0)
        top = ref[t, :half, :half] - product(corner, ratio, 1, 1)
        ref[t, :half, :half] = top * across[:, :half] * down[:half]
        ref[t, :half, half:] = corner * across[:, half:] * down[:half]
        ref[t, half:, :half] = corner.T * across[:, :half] * down[half:]
        ref[t, half:, half:] = trailing[t] * across[:, half:] * down[half:]


def gradients(source, target, observed, upper, lower):
    row = lax.broadcasted_iota(jnp.int32, observed.shape, 0)
    mask = jnp.where(row < observed.shape[0] // 2, upper, lower).astype(jnp.float32)
    residual = mask * (product(source, target, 1, 1) - observed)
    return product(residual, target, 1, 0), product(residual, source, 0, 0)


def diagonal(square):
    row, col = grid_of(square.shape)
    return jnp.sum(jnp.where(row == col, square, 0.0), axis=0, keepdims=True)


def first_kernel(tiles, source_ref, target_ref, observed_ref, grad_ref, moving_ref, sums_ref):
    source, target = source_ref[...], target_ref[...]
    count = target.shape[0]
    grad_source, grad_target = gradients(source, target, observed_ref[0], tiles[0, 0], tiles[0, 1])
    grad_ref[...] = grad_source
    moving_ref[:count, :] = target
    moving_ref[count:, :] = grad_target
    gram_source = product(source, source, 0, 0)
    gram_target = product(target, target, 0, 0)
    cross = product(source, grad_source, 0, 0)
    square_source = product(grad_source, grad_source, 0, 0)
    square_target = product(grad_target, grad_target, 0, 0)
    row, col = grid_of(cross.shape)
    upper = row <= col
    packed = (
        cross,
        jnp.where(upper, gram_source, gram_target),
        jnp.where(upper, square_source, square_target),
    )
    for place, square in enumerate(packed):
        for side in range(2):
            rows = slice(16 * place + 8 * side, 16 * place + 8 * side + 8)
            sums_ref[:, rows, :] = square[:, 128 * side : 128 * side + 128].reshape(PIECES, 8, 128)
    sums_ref[:, 48:56, :] = jnp.zeros((PIECES, 8, 128), jnp.float32)
    for place, square in enumerate((gram_target, square_target)):
        line = diagonal(square)
        for side in range(2):
            slot = 48 + 2 * place + side
            sums_ref[0, slot : slot + 1, :] = line[:, 128 * side : 128 * side + 128]


def unpacked(sums_ref, place):
    halves = [sums_ref[:, 16 * place + 8 * side : 16 * place + 8 * side + 8, :].reshape(256, 128) for side in range(2)]
    return jnp.concatenate(halves, 1)


def unpacked_pair(sums_ref, place):
    packed = unpacked(sums_ref, place)
    flipped = packed.T
    row, col = grid_of(packed.shape)
    line = jnp.concatenate([sums_ref[0, 46 + 2 * place + side : 47 + 2 * place + side, :] for side in range(2)], 1)
    first = jnp.where(row <= col, packed, flipped)
    second = jnp.where(row > col, packed, flipped)
    return first, jnp.where(row == col, line, second)


def updated_gram(gram, cross, square, inverse):
    moved = product(cross, inverse, 1, 0)
    twice = product(product(inverse, square, 1, 0), inverse, 1, 0)
    return gram - step_size * (moved + moved.T) + (step_size * step_size) * twice


def inverse_kernel(source_rows, target_rows, sums_ref, gram_out, inverse_out):
    gram_out[0], gram_out[1] = unpacked_pair(sums_ref, 1)
    inverse_out[0] = gram_out[0] / source_rows
    inverse_out[1] = gram_out[1] / target_rows
    invert_pair(inverse_out)


def second_kernel(
    source_rows, target_rows,
    tiles, sums_ref, gram_ref, inverse_ref, source_ref, grad_ref, moving_ref, observed_ref,
    source_out, grad_out, moving_out, gram_out,
):
    count = moving_ref.shape[0] // 2
    source = source_ref[...] - step_size * product(grad_ref[...], inverse_ref[1], 1, 0)
    target = moving_ref[:count, :] - step_size * product(moving_ref[count:, :], inverse_ref[0], 1, 0)
    source_out[...] = source
    moving_out[:count, :] = target
    grad_source, grad_target = gradients(source, target, observed_ref[1], tiles[1, 0], tiles[1, 1])
    grad_out[...] = grad_source
    moving_out[count:, :] = grad_target
    square_source, square_target = unpacked_pair(sums_ref, 2)
    cross = unpacked(sums_ref, 0)
    gram_out[0] = updated_gram(gram_ref[0], cross, square_source, inverse_ref[1]) / source_rows
    gram_out[1] = updated_gram(gram_ref[1], cross.T, square_target, inverse_ref[0]) / target_rows


def third_kernel(gram_ref, source_ref, grad_ref, source_out, inverse_out, work):
    work[...] = gram_ref[...]
    invert_pair(work)
    source_out[...] = source_ref[...] - step_size * product(grad_ref[...], work[1], 1, 0)
    inverse_out[...] = work[0]


def call(kernel, shapes, scratch, *arguments, scalars=0):
    vmem = pl.BlockSpec(memory_space=pltpu.VMEM)
    smem = pl.BlockSpec(memory_space=pltpu.SMEM)
    return pl.pallas_call(
        kernel,
        out_shape=[jax.ShapeDtypeStruct(shape, jnp.float32) for shape in shapes],
        in_specs=[smem] * scalars + [vmem] * (len(arguments) - scalars),
        out_specs=[vmem] * len(shapes),
        scratch_shapes=[pltpu.VMEM(shape, jnp.float32) for shape in scratch],
    )(*arguments)


def next_position(value):
    count = lax.axis_size(WIDE)
    return lax.ppermute(value, WIDE, [(place, (place + 1) % count) for place in range(count)])


def exchanged(value, axes):
    return lax.all_to_all(value, axes, 0, 0, tiled=True)


def spread(value, axes):
    return exchanged(jnp.broadcast_to(value[None], (lax.axis_size(axes), *value.shape)), axes)


def on_device(source, target, observed, tiles):
    devices = lax.axis_size(AXES)
    source_rows = source.shape[0] * devices
    target_rows = target.shape[0] * devices
    flags = tiles.reshape(2, 2)
    square = (256, 256)
    grad, moving, sums = call(
        first_kernel, (square, square, (PIECES, 56, 128)), (), flags, source, target, observed, scalars=1
    )
    sums = jnp.sum(exchanged(sums, SCATTER), axis=0)
    sums = jnp.sum(spread(sums, EXCHANGE), axis=0)
    sums, moving = lax.optimization_barrier((spread(sums, SCATTER), moving))
    moving = next_position(moving)

    def inverses(*refs):
        inverse_kernel(source_rows, target_rows, *refs)

    def middle(*refs):
        second_kernel(source_rows, target_rows, *refs)

    pair = (2, *square)
    grams, inverse = call(inverses, (pair, pair), (), sums)
    source, grad, moving, grams = call(
        middle, (square, square, square, pair), (),
        flags, sums, grams, inverse, source, grad, moving, observed, scalars=1,
    )
    moving = next_position(moving)
    source, inverse = call(third_kernel, (square, square), ((2, *square),), grams, source, grad)
    count = target.shape[0]
    target = moving[:count] - step_size * product(moving[count:], inverse, 1, 0)
    return source, target


def solution(mesh):
    fine = Mesh(mesh.devices.reshape((2,) * len(AXES)), AXES)
    placed = (P(AXES, None), P(AXES, None), P(None, AXES, None), P(None, AXES, None))
    return jax.shard_map(
        on_device, mesh=fine, in_specs=placed, out_specs=(P(AXES, None), P(AXES, None)), check_vma=False
    )
```

```python
import jax
import jax.numpy as jnp
from jax import lax
from jax.experimental import pallas as pl
from jax.experimental.pallas import tpu as pltpu
from jax.sharding import Mesh
from jax.sharding import PartitionSpec as P

step_size = 0.0002

AXES = ("xh", "xl", "ya", "yb", "yc", "zh", "zla", "zlb", "core")
WIDE = ("xh", "xl", "ya", "yb", "yc", "zh")
NEAR = ("xh", "xl", "yc", "zlb")
FAR = (("ya", "yb"), ("zh", "zla"))
PIECES = 32
BLOCK = 64


def product(left, right, left_dim, right_dim):
    return lax.dot_general(
        left,
        right,
        (((left_dim,), (right_dim,)), ((), ())),
        precision=lax.Precision.HIGHEST,
        preferred_element_type=jnp.float32,
    )


def grid_of(shape):
    return lax.broadcasted_iota(jnp.int32, shape, 0), lax.broadcasted_iota(jnp.int32, shape, 1)


def sweep_pair(panels, first):
    rows, cols = panels[0].shape
    sub, lane = grid_of((8, cols))
    if first:
        panels = [pltpu.roll(panel, cols - first, 1) for panel in panels]
    start = tuple(tuple(panel[8 * g : 8 * g + 8] for g in range(rows // 8)) for panel in panels)

    def wide(value):
        return jnp.broadcast_to(value, (8, cols))

    def eight_pivots(_, carry):
        held = [list(groups) for groups in carry]
        for r in range(0, 8, 2):
            here, after = lane == r, lane == r + 1
            for t, groups in enumerate(held):
                left = [wide(group[:, r : r + 1]) for group in groups]
                right = [wide(group[:, r + 1 : r + 2]) for group in groups]
                upper = jnp.where(after, 0.0, jnp.where(here, 1.0, wide(groups[0][r : r + 1])))
                lower = jnp.where(here, 0.0, jnp.where(after, 1.0, wide(groups[0][r + 1 : r + 2])))
                main = jnp.where(sub == r, left[0], right[0])
                cross = wide(jnp.where(sub == r, right[0], left[0])[r : r + 1])
                first_pivot, second_pivot = wide(main[r : r + 1]), wide(main[r + 1 : r + 2])
                scale = 1.0 / (first_pivot * second_pivot - cross * cross)
                upper, lower = (
                    scale * (second_pivot * upper - cross * lower),
                    scale * (first_pivot * lower - cross * upper),
                )
                swept = [
                    jnp.where(here | after, 0.0, group) - left[g] * upper - right[g] * lower
                    for g, group in enumerate(groups)
                ]
                swept[0] = jnp.where(sub == r, upper, jnp.where(sub == r + 1, lower, swept[0]))
                held[t] = swept
        return tuple(tuple(pltpu.roll(group, cols - 8, 1) for group in groups[1:] + groups[:1]) for groups in held)

    swept = [jnp.concatenate(groups, 0) for groups in lax.fori_loop(0, rows // 8, eight_pivots, start)]
    back = (first + rows) % cols
    return [pltpu.roll(panel, back, 1) for panel in swept] if back else swept


def invert_blocks(squares):
    size = squares[0].shape[0]
    lane = lax.broadcasted_iota(jnp.int32, (BLOCK, size), 1)
    panels = [[square[start : start + BLOCK] for start in range(0, size, BLOCK)] for square in squares]
    for block in range(size // BLOCK):
        start = block * BLOCK
        swept = sweep_pair([held[block] for held in panels], start)
        inside = (lane >= start) & (lane < start + BLOCK)
        for held, panel in zip(panels, swept):
            for other in range(len(held)):
                left = held[other][:, start : start + BLOCK]
                if other != block:
                    held[other] = jnp.where(inside, 0.0, held[other]) - product(left, panel, 1, 0)
            held[block] = panel
    return [jnp.concatenate(held, 0) for held in panels]


def invert_pair(ref):
    size = ref.shape[1]
    half = size // 2
    row, col = grid_of((size, size))
    scales = []
    for t in range(2):
        whole = ref[t]
        main = jnp.where(row == col, whole, 0.0)
        across = lax.rsqrt(jnp.sum(main, axis=0, keepdims=True))
        down = lax.rsqrt(jnp.sum(main, axis=1, keepdims=True))
        scales.append((across, down))
        ref[t] = whole * across * down
    leading = invert_blocks([ref[t, :half, :half] for t in range(2)])
    ratio = [product(leading[t], ref[t, :half, half:], 1, 0) for t in range(2)]
    rest = [ref[t, half:, half:] - product(ref[t, :half, half:], ratio[t], 0, 0) for t in range(2)]
    for t in range(2):
        ref[t, :half, :half] = leading[t]
        ref[t, :half, half:] = ratio[t]
    trailing = invert_blocks(rest)
    for t in range(2):
        across, down = scales[t]
        ratio = ref[t, :half, half:]
        corner = -product(ratio, trailing[t], 1, 0)
        top = ref[t, :half, :half] - product(corner, ratio, 1, 1)
        ref[t, :half, :half] = top * across[:, :half] * down[:half]
        ref[t, :half, half:] = corner * across[:, half:] * down[:half]
        ref[t, half:, :half] = corner.T * across[:, :half] * down[half:]
        ref[t, half:, half:] = trailing[t] * across[:, half:] * down[half:]


def gradients(source, target, observed, upper, lower):
    row = lax.broadcasted_iota(jnp.int32, observed.shape, 0)
    mask = jnp.where(row < observed.shape[0] // 2, upper, lower).astype(jnp.float32)
    residual = mask * (product(source, target, 1, 1) - observed)
    return product(residual, target, 1, 0), product(residual, source, 0, 0)


def diagonal(square):
    row, col = grid_of(square.shape)
    return jnp.sum(jnp.where(row == col, square, 0.0), axis=0, keepdims=True)


def first_kernel(tiles, source_ref, target_ref, observed_ref, grad_ref, moving_ref, sums_ref):
    source, target = source_ref[...], target_ref[...]
    count = target.shape[0]
    grad_source, grad_target = gradients(source, target, observed_ref[0], tiles[0, 0], tiles[0, 1])
    grad_ref[...] = grad_source
    moving_ref[:count, :] = target
    moving_ref[count:, :] = grad_target
    gram_source = product(source, source, 0, 0)
    gram_target = product(target, target, 0, 0)
    cross = product(source, grad_source, 0, 0)
    square_source = product(grad_source, grad_source, 0, 0)
    square_target = product(grad_target, grad_target, 0, 0)
    row, col = grid_of(cross.shape)
    upper = row <= col
    packed = (
        cross,
        jnp.where(upper, gram_source, gram_target),
        jnp.where(upper, square_source, square_target),
    )
    for place, square in enumerate(packed):
        for side in range(2):
            rows = slice(16 * place + 8 * side, 16 * place + 8 * side + 8)
            sums_ref[:, rows, :] = square[:, 128 * side : 128 * side + 128].reshape(PIECES, 8, 128)
    sums_ref[:, 48:56, :] = jnp.zeros((PIECES, 8, 128), jnp.float32)
    for place, square in enumerate((gram_target, square_target)):
        line = diagonal(square)
        for side in range(2):
            slot = 48 + 2 * place + side
            sums_ref[0, slot : slot + 1, :] = line[:, 128 * side : 128 * side + 128]


def unpacked(sums_ref, place):
    halves = [sums_ref[:, 16 * place + 8 * side : 16 * place + 8 * side + 8, :].reshape(256, 128) for side in range(2)]
    return jnp.concatenate(halves, 1)


def unpacked_pair(sums_ref, place):
    packed = unpacked(sums_ref, place)
    flipped = packed.T
    row, col = grid_of(packed.shape)
    line = jnp.concatenate([sums_ref[0, 46 + 2 * place + side : 47 + 2 * place + side, :] for side in range(2)], 1)
    first = jnp.where(row <= col, packed, flipped)
    second = jnp.where(row > col, packed, flipped)
    return first, jnp.where(row == col, line, second)


def updated_gram(gram, cross, square, inverse):
    moved = product(cross, inverse, 1, 0)
    twice = product(product(inverse, square, 1, 0), inverse, 1, 0)
    return gram - step_size * (moved + moved.T) + (step_size * step_size) * twice


def inverse_kernel(source_rows, target_rows, sums_ref, gram_out, inverse_out):
    gram_out[0], gram_out[1] = unpacked_pair(sums_ref, 1)
    inverse_out[0] = gram_out[0] / source_rows
    inverse_out[1] = gram_out[1] / target_rows
    invert_pair(inverse_out)


def second_kernel(
    source_rows, target_rows,
    tiles, sums_ref, gram_ref, inverse_ref, source_ref, grad_ref, moving_ref, observed_ref,
    source_out, grad_out, moving_out, gram_out,
):
    count = moving_ref.shape[0] // 2
    source = source_ref[...] - step_size * product(grad_ref[...], inverse_ref[1], 1, 0)
    target = moving_ref[:count, :] - step_size * product(moving_ref[count:, :], inverse_ref[0], 1, 0)
    source_out[...] = source
    moving_out[:count, :] = target
    grad_source, grad_target = gradients(source, target, observed_ref[1], tiles[1, 0], tiles[1, 1])
    grad_out[...] = grad_source
    moving_out[count:, :] = grad_target
    square_source, square_target = unpacked_pair(sums_ref, 2)
    cross = unpacked(sums_ref, 0)
    gram_out[0] = updated_gram(gram_ref[0], cross, square_source, inverse_ref[1]) / source_rows
    gram_out[1] = updated_gram(gram_ref[1], cross.T, square_target, inverse_ref[0]) / target_rows


def third_kernel(gram_ref, source_ref, grad_ref, source_out, inverse_out, work):
    work[...] = gram_ref[...]
    invert_pair(work)
    source_out[...] = source_ref[...] - step_size * product(grad_ref[...], work[1], 1, 0)
    inverse_out[...] = work[0]


def call(kernel, shapes, scratch, *arguments, scalars=0):
    vmem = pl.BlockSpec(memory_space=pltpu.VMEM)
    smem = pl.BlockSpec(memory_space=pltpu.SMEM)
    return pl.pallas_call(
        kernel,
        out_shape=[jax.ShapeDtypeStruct(shape, jnp.float32) for shape in shapes],
        in_specs=[smem] * scalars + [vmem] * (len(arguments) - scalars),
        out_specs=[vmem] * len(shapes),
        scratch_shapes=[pltpu.VMEM(shape, jnp.float32) for shape in scratch],
    )(*arguments)


def next_position(value):
    count = lax.axis_size(WIDE)
    return lax.ppermute(value, WIDE, [(place, (place + 1) % count) for place in range(count)])


def exchanged(value, axes):
    return lax.all_to_all(value, axes, 0, 0, tiled=True)


def spread(value, axes):
    return exchanged(jnp.broadcast_to(value[None], (lax.axis_size(axes), *value.shape)), axes)


def on_device(source, target, observed, tiles):
    devices = lax.axis_size(AXES)
    source_rows = source.shape[0] * devices
    target_rows = target.shape[0] * devices
    flags = tiles.reshape(2, 2)
    square = (256, 256)
    grad, moving, sums = call(
        first_kernel, (square, square, (PIECES, 56, 128)), (), flags, source, target, observed, scalars=1
    )
    shape = sums.shape
    sums = jnp.sum(exchanged(sums.reshape(2, -1, 128), "core"), axis=0)
    sums = jnp.sum(exchanged(sums.reshape(-1, *shape[1:]), NEAR), axis=0)
    for axes in FAR:
        sums = jnp.sum(spread(sums, axes), axis=0)
    sums = spread(sums, NEAR).reshape(-1, 128)
    sums, moving = lax.optimization_barrier((spread(sums, "core").reshape(shape), moving))
    moving = next_position(moving)

    def inverses(*refs):
        inverse_kernel(source_rows, target_rows, *refs)

    def middle(*refs):
        second_kernel(source_rows, target_rows, *refs)

    pair = (2, *square)
    grams, inverse = call(inverses, (pair, pair), (), sums)
    source, grad, moving, grams = call(
        middle, (square, square, square, pair), (),
        flags, sums, grams, inverse, source, grad, moving, observed, scalars=1,
    )
    moving = next_position(moving)
    source, inverse = call(third_kernel, (square, square), ((2, *square),), grams, source, grad)
    count = target.shape[0]
    target = moving[:count] - step_size * product(moving[count:], inverse, 1, 0)
    return source, target


def solution(mesh):
    fine = Mesh(mesh.devices.reshape((2,) * len(AXES)), AXES)
    placed = (P(AXES, None), P(AXES, None), P(None, AXES, None), P(None, AXES, None))
    return jax.shard_map(
        on_device, mesh=fine, in_specs=placed, out_specs=(P(AXES, None), P(AXES, None)), check_vma=False
    )
```

```python
import jax
import jax.numpy as jnp
from jax import lax
from jax.experimental import pallas as pl
from jax.experimental.pallas import tpu as pltpu
from jax.sharding import Mesh
from jax.sharding import PartitionSpec as P

step_size = 0.0002

AXES = ("xh", "xl", "ya", "yb", "yc", "zh", "zla", "zlb", "core")
WIDE = ("xh", "xl", "ya", "yb", "yc", "zh")
NEAR = ("xh", "xl", "yc", "zlb")
FAR = (("ya", "yb"), ("zh", "zla"))
PIECES = 32
BLOCK = 64
TURNS = 4
RESIDUAL = 0.003


def product(left, right, left_dim, right_dim, precision=lax.Precision.HIGHEST):
    return lax.dot_general(
        left,
        right,
        (((left_dim,), (right_dim,)), ((), ())),
        precision=precision,
        preferred_element_type=jnp.float32,
    )


def grid_of(shape):
    return lax.broadcasted_iota(jnp.int32, shape, 0), lax.broadcasted_iota(jnp.int32, shape, 1)


def sweep_pair(panels, first):
    rows, cols = panels[0].shape
    sub, lane = grid_of((8, cols))
    if first:
        panels = [pltpu.roll(panel, cols - first, 1) for panel in panels]
    start = tuple(tuple(panel[8 * g : 8 * g + 8] for g in range(rows // 8)) for panel in panels)

    def wide(value):
        return jnp.broadcast_to(value, (8, cols))

    def eight_pivots(_, carry):
        held = [list(groups) for groups in carry]
        for r in range(0, 8, 2):
            here, after = lane == r, lane == r + 1
            for t, groups in enumerate(held):
                left = [wide(group[:, r : r + 1]) for group in groups]
                right = [wide(group[:, r + 1 : r + 2]) for group in groups]
                upper = jnp.where(after, 0.0, jnp.where(here, 1.0, wide(groups[0][r : r + 1])))
                lower = jnp.where(here, 0.0, jnp.where(after, 1.0, wide(groups[0][r + 1 : r + 2])))
                main = jnp.where(sub == r, left[0], right[0])
                cross = wide(jnp.where(sub == r, right[0], left[0])[r : r + 1])
                first_pivot, second_pivot = wide(main[r : r + 1]), wide(main[r + 1 : r + 2])
                scale = 1.0 / (first_pivot * second_pivot - cross * cross)
                upper, lower = (
                    scale * (second_pivot * upper - cross * lower),
                    scale * (first_pivot * lower - cross * upper),
                )
                swept = [
                    jnp.where(here | after, 0.0, group) - left[g] * upper - right[g] * lower
                    for g, group in enumerate(groups)
                ]
                swept[0] = jnp.where(sub == r, upper, jnp.where(sub == r + 1, lower, swept[0]))
                held[t] = swept
        return tuple(tuple(pltpu.roll(group, cols - 8, 1) for group in groups[1:] + groups[:1]) for groups in held)

    swept = [jnp.concatenate(groups, 0) for groups in lax.fori_loop(0, rows // 8, eight_pivots, start)]
    back = (first + rows) % cols
    return [pltpu.roll(panel, back, 1) for panel in swept] if back else swept


def invert_blocks(squares):
    size = squares[0].shape[0]
    lane = lax.broadcasted_iota(jnp.int32, (BLOCK, size), 1)
    panels = [[square[start : start + BLOCK] for start in range(0, size, BLOCK)] for square in squares]
    for block in range(size // BLOCK):
        start = block * BLOCK
        swept = sweep_pair([held[block] for held in panels], start)
        inside = (lane >= start) & (lane < start + BLOCK)
        for held, panel in zip(panels, swept):
            for other in range(len(held)):
                left = held[other][:, start : start + BLOCK]
                if other != block:
                    held[other] = jnp.where(inside, 0.0, held[other]) - product(left, panel, 1, 0)
            held[block] = panel
    return [jnp.concatenate(held, 0) for held in panels]


def invert_pair(ref):
    size = ref.shape[1]
    half = size // 2
    row, col = grid_of((size, size))
    scales = []
    for t in range(2):
        whole = ref[t]
        main = jnp.where(row == col, whole, 0.0)
        across = lax.rsqrt(jnp.sum(main, axis=0, keepdims=True))
        down = lax.rsqrt(jnp.sum(main, axis=1, keepdims=True))
        scales.append((across, down))
        ref[t] = whole * across * down
    leading = invert_blocks([ref[t, :half, :half] for t in range(2)])
    ratio = [product(leading[t], ref[t, :half, half:], 1, 0) for t in range(2)]
    rest = [ref[t, half:, half:] - product(ref[t, :half, half:], ratio[t], 0, 0) for t in range(2)]
    for t in range(2):
        ref[t, :half, :half] = leading[t]
        ref[t, :half, half:] = ratio[t]
    trailing = invert_blocks(rest)
    for t in range(2):
        across, down = scales[t]
        ratio = ref[t, :half, half:]
        corner = -product(ratio, trailing[t], 1, 0)
        top = ref[t, :half, :half] - product(corner, ratio, 1, 1)
        ref[t, :half, :half] = top * across[:, :half] * down[:half]
        ref[t, :half, half:] = corner * across[:, half:] * down[:half]
        ref[t, half:, :half] = corner.T * across[:, :half] * down[half:]
        ref[t, half:, half:] = trailing[t] * across[:, half:] * down[half:]


def gradients(source, target, observed, upper, lower):
    row = lax.broadcasted_iota(jnp.int32, observed.shape, 0)
    mask = jnp.where(row < observed.shape[0] // 2, upper, lower).astype(jnp.float32)
    residual = mask * (product(source, target, 1, 1) - observed)
    return product(residual, target, 1, 0), product(residual, source, 0, 0)


def diagonal(square):
    row, col = grid_of(square.shape)
    return jnp.sum(jnp.where(row == col, square, 0.0), axis=0, keepdims=True)


def first_kernel(tiles, source_ref, target_ref, observed_ref, grad_ref, moving_ref, sums_ref):
    source, target = source_ref[...], target_ref[...]
    count = target.shape[0]
    grad_source, grad_target = gradients(source, target, observed_ref[0], tiles[0, 0], tiles[0, 1])
    grad_ref[...] = grad_source
    moving_ref[:count, :] = target
    moving_ref[count:, :] = grad_target
    gram_source = product(source, source, 0, 0)
    gram_target = product(target, target, 0, 0)
    cross = product(source, grad_source, 0, 0)
    square_source = product(grad_source, grad_source, 0, 0)
    square_target = product(grad_target, grad_target, 0, 0)
    row, col = grid_of(cross.shape)
    upper = row <= col
    packed = (
        cross,
        jnp.where(upper, gram_source, gram_target),
        jnp.where(upper, square_source, square_target),
    )
    for place, square in enumerate(packed):
        for side in range(2):
            rows = slice(16 * place + 8 * side, 16 * place + 8 * side + 8)
            sums_ref[:, rows, :] = square[:, 128 * side : 128 * side + 128].reshape(PIECES, 8, 128)
    sums_ref[:, 48:56, :] = jnp.zeros((PIECES, 8, 128), jnp.float32)
    for place, square in enumerate((gram_target, square_target)):
        line = diagonal(square)
        for side in range(2):
            slot = 48 + 2 * place + side
            sums_ref[0, slot : slot + 1, :] = line[:, 128 * side : 128 * side + 128]


def unpacked(sums_ref, place):
    halves = [sums_ref[:, 16 * place + 8 * side : 16 * place + 8 * side + 8, :].reshape(256, 128) for side in range(2)]
    return jnp.concatenate(halves, 1)


def unpacked_pair(sums_ref, place):
    packed = unpacked(sums_ref, place)
    flipped = packed.T
    row, col = grid_of(packed.shape)
    line = jnp.concatenate([sums_ref[0, 46 + 2 * place + side : 47 + 2 * place + side, :] for side in range(2)], 1)
    first = jnp.where(row <= col, packed, flipped)
    second = jnp.where(row > col, packed, flipped)
    return first, jnp.where(row == col, line, second)


def updated_gram(gram, cross, square, inverse):
    moved = product(cross, inverse, 1, 0)
    twice = product(product(inverse, square, 1, 0), inverse, 1, 0)
    return gram - step_size * (moved + moved.T) + (step_size * step_size) * twice


def inverse_kernel(source_rows, target_rows, sums_ref, gram_out, inverse_out):
    gram_out[0], gram_out[1] = unpacked_pair(sums_ref, 1)
    inverse_out[0] = gram_out[0] / source_rows
    inverse_out[1] = gram_out[1] / target_rows
    invert_pair(inverse_out)


def second_kernel(
    source_rows, target_rows,
    tiles, sums_ref, gram_ref, inverse_ref, source_ref, grad_ref, moving_ref, observed_ref,
    source_out, grad_out, moving_out, gram_out,
):
    count = moving_ref.shape[0] // 2
    source = source_ref[...] - step_size * product(grad_ref[...], inverse_ref[1], 1, 0)
    target = moving_ref[:count, :] - step_size * product(moving_ref[count:, :], inverse_ref[0], 1, 0)
    source_out[...] = source
    moving_out[:count, :] = target
    grad_source, grad_target = gradients(source, target, observed_ref[1], tiles[1, 0], tiles[1, 1])
    grad_out[...] = grad_source
    moving_out[count:, :] = grad_target
    square_source, square_target = unpacked_pair(sums_ref, 2)
    cross = unpacked(sums_ref, 0)
    gram_out[0] = updated_gram(gram_ref[0], cross, square_source, inverse_ref[1]) / source_rows
    gram_out[1] = updated_gram(gram_ref[1], cross.T, square_target, inverse_ref[0]) / target_rows


def invert_pair_from(gram_ref, guess_ref, inverse_ref, error_ref):
    size = gram_ref.shape[1]
    row, col = grid_of((size, size))

    def residual():
        total = 0.0
        for t in range(2):
            error = jnp.where(row == col, 1.0, 0.0) - product(gram_ref[t], inverse_ref[t], 1, 0)
            error_ref[t] = error
            total += jnp.sum(error * error)
        return total

    def refine():
        for t in range(2):
            error = error_ref[t]
            error += product(error, error, 1, 0, lax.Precision.DEFAULT)
            inverse_ref[t] += product(inverse_ref[t], error, 1, 0)

    def turn(state):
        refine()
        return state[0] + 1, residual()

    inverse_ref[...] = guess_ref[...]
    _, total = lax.while_loop(
        lambda state: (state[0] < TURNS) & (state[1] > RESIDUAL * RESIDUAL), turn, (0, residual())
    )
    settled = total <= RESIDUAL * RESIDUAL

    @pl.when(settled)
    def _():
        refine()

    @pl.when(jnp.logical_not(settled))
    def _():
        inverse_ref[...] = gram_ref[...]
        invert_pair(inverse_ref)


def third_kernel(gram_ref, guess_ref, source_ref, grad_ref, source_out, inverse_out, work, error):
    invert_pair_from(gram_ref, guess_ref, work, error)
    source_out[...] = source_ref[...] - step_size * product(grad_ref[...], work[1], 1, 0)
    inverse_out[...] = work[0]


def call(kernel, shapes, scratch, *arguments, scalars=0):
    vmem = pl.BlockSpec(memory_space=pltpu.VMEM)
    smem = pl.BlockSpec(memory_space=pltpu.SMEM)
    return pl.pallas_call(
        kernel,
        out_shape=[jax.ShapeDtypeStruct(shape, jnp.float32) for shape in shapes],
        in_specs=[smem] * scalars + [vmem] * (len(arguments) - scalars),
        out_specs=[vmem] * len(shapes),
        scratch_shapes=[pltpu.VMEM(shape, jnp.float32) for shape in scratch],
    )(*arguments)


def next_position(value):
    count = lax.axis_size(WIDE)
    return lax.ppermute(value, WIDE, [(place, (place + 1) % count) for place in range(count)])


def exchanged(value, axes):
    return lax.all_to_all(value, axes, 0, 0, tiled=True)


def spread(value, axes):
    return exchanged(jnp.broadcast_to(value[None], (lax.axis_size(axes), *value.shape)), axes)


def on_device(source, target, observed, tiles):
    devices = lax.axis_size(AXES)
    source_rows = source.shape[0] * devices
    target_rows = target.shape[0] * devices
    flags = tiles.reshape(2, 2)
    square = (256, 256)
    grad, moving, sums = call(
        first_kernel, (square, square, (PIECES, 56, 128)), (), flags, source, target, observed, scalars=1
    )
    shape = sums.shape
    sums = jnp.sum(exchanged(sums.reshape(2, -1, 128), "core"), axis=0)
    sums = jnp.sum(exchanged(sums.reshape(-1, *shape[1:]), NEAR), axis=0)
    for axes in FAR:
        sums = jnp.sum(spread(sums, axes), axis=0)
    sums = spread(sums, NEAR).reshape(-1, 128)
    sums, moving = lax.optimization_barrier((spread(sums, "core").reshape(shape), moving))
    moving = next_position(moving)

    def inverses(*refs):
        inverse_kernel(source_rows, target_rows, *refs)

    def middle(*refs):
        second_kernel(source_rows, target_rows, *refs)

    pair = (2, *square)
    grams, inverse = call(inverses, (pair, pair), (), sums)
    source, grad, moving, grams = call(
        middle, (square, square, square, pair), (),
        flags, sums, grams, inverse, source, grad, moving, observed, scalars=1,
    )
    moving = next_position(moving)
    source, inverse = call(third_kernel, (square, square), (pair, pair), grams, inverse, source, grad)
    count = target.shape[0]
    target = moving[:count] - step_size * product(moving[count:], inverse, 1, 0)
    return source, target


def solution(mesh):
    fine = Mesh(mesh.devices.reshape((2,) * len(AXES)), AXES)
    placed = (P(AXES, None), P(AXES, None), P(None, AXES, None), P(None, AXES, None))
    return jax.shard_map(
        on_device, mesh=fine, in_specs=placed, out_specs=(P(AXES, None), P(AXES, None)), check_vma=False
    )
```

```python
import jax
import jax.numpy as jnp
from jax import lax
from jax.experimental import pallas as pl
from jax.experimental.pallas import tpu as pltpu
from jax.sharding import Mesh
from jax.sharding import PartitionSpec as P

step_size = 0.0002

AXES = ("xh", "xl", "ya", "yb", "yc", "zh", "zla", "zlb", "core")
WIDE = ("xh", "xl", "ya", "yb", "yc", "zh")
NEAR = ("xh", "xl", "yc", "zlb")
FAR = (("ya", "yb"), ("zh", "zla"))
PIECES = 32
BLOCK = 64
TURNS = 4
RESIDUAL = 0.003


def product(left, right, left_dim, right_dim, precision=lax.Precision.HIGHEST):
    return lax.dot_general(
        left,
        right,
        (((left_dim,), (right_dim,)), ((), ())),
        precision=precision,
        preferred_element_type=jnp.float32,
    )


def grid_of(shape):
    return lax.broadcasted_iota(jnp.int32, shape, 0), lax.broadcasted_iota(jnp.int32, shape, 1)


def sweep_pair(panels, first):
    rows, cols = panels[0].shape
    sub, lane = grid_of((8, cols))
    if first:
        panels = [pltpu.roll(panel, cols - first, 1) for panel in panels]
    start = tuple(tuple(panel[8 * g : 8 * g + 8] for g in range(rows // 8)) for panel in panels)

    def wide(value):
        return jnp.broadcast_to(value, (8, cols))

    def eight_pivots(_, carry):
        held = [list(groups) for groups in carry]
        for r in range(0, 8, 2):
            here, after = lane == r, lane == r + 1
            for t, groups in enumerate(held):
                left = [wide(group[:, r : r + 1]) for group in groups]
                right = [wide(group[:, r + 1 : r + 2]) for group in groups]
                upper = jnp.where(after, 0.0, jnp.where(here, 1.0, wide(groups[0][r : r + 1])))
                lower = jnp.where(here, 0.0, jnp.where(after, 1.0, wide(groups[0][r + 1 : r + 2])))
                main = jnp.where(sub == r, left[0], right[0])
                cross = wide(jnp.where(sub == r, right[0], left[0])[r : r + 1])
                first_pivot, second_pivot = wide(main[r : r + 1]), wide(main[r + 1 : r + 2])
                scale = 1.0 / (first_pivot * second_pivot - cross * cross)
                upper, lower = (
                    scale * (second_pivot * upper - cross * lower),
                    scale * (first_pivot * lower - cross * upper),
                )
                swept = [
                    jnp.where(here | after, 0.0, group) - left[g] * upper - right[g] * lower
                    for g, group in enumerate(groups)
                ]
                swept[0] = jnp.where(sub == r, upper, jnp.where(sub == r + 1, lower, swept[0]))
                held[t] = swept
        return tuple(tuple(pltpu.roll(group, cols - 8, 1) for group in groups[1:] + groups[:1]) for groups in held)

    swept = [jnp.concatenate(groups, 0) for groups in lax.fori_loop(0, rows // 8, eight_pivots, start)]
    back = (first + rows) % cols
    return [pltpu.roll(panel, back, 1) for panel in swept] if back else swept


def invert_blocks(squares):
    size = squares[0].shape[0]
    lane = lax.broadcasted_iota(jnp.int32, (BLOCK, size), 1)
    panels = [[square[start : start + BLOCK] for start in range(0, size, BLOCK)] for square in squares]
    for block in range(size // BLOCK):
        start = block * BLOCK
        swept = sweep_pair([held[block] for held in panels], start)
        inside = (lane >= start) & (lane < start + BLOCK)
        for held, panel in zip(panels, swept):
            for other in range(len(held)):
                left = held[other][:, start : start + BLOCK]
                if other != block:
                    held[other] = jnp.where(inside, 0.0, held[other]) - product(left, panel, 1, 0)
            held[block] = panel
    return [jnp.concatenate(held, 0) for held in panels]


def invert_pair(ref):
    size = ref.shape[1]
    half = size // 2
    row, col = grid_of((size, size))
    scales = []
    for t in range(2):
        whole = ref[t]
        main = jnp.where(row == col, whole, 0.0)
        across = lax.rsqrt(jnp.sum(main, axis=0, keepdims=True))
        down = lax.rsqrt(jnp.sum(main, axis=1, keepdims=True))
        scales.append((across, down))
        ref[t] = whole * across * down
    leading = invert_blocks([ref[t, :half, :half] for t in range(2)])
    ratio = [product(leading[t], ref[t, :half, half:], 1, 0) for t in range(2)]
    rest = [ref[t, half:, half:] - product(ref[t, :half, half:], ratio[t], 0, 0) for t in range(2)]
    for t in range(2):
        ref[t, :half, :half] = leading[t]
        ref[t, :half, half:] = ratio[t]
    trailing = invert_blocks(rest)
    for t in range(2):
        across, down = scales[t]
        ratio = ref[t, :half, half:]
        corner = -product(ratio, trailing[t], 1, 0)
        top = ref[t, :half, :half] - product(corner, ratio, 1, 1)
        ref[t, :half, :half] = top * across[:, :half] * down[:half]
        ref[t, :half, half:] = corner * across[:, half:] * down[:half]
        ref[t, half:, :half] = corner.T * across[:, :half] * down[half:]
        ref[t, half:, half:] = trailing[t] * across[:, half:] * down[half:]


def masked_residual(source, target, observed, upper, lower):
    row = lax.broadcasted_iota(jnp.int32, observed.shape, 0)
    mask = jnp.where(row < observed.shape[0] // 2, upper, lower).astype(jnp.float32)
    return mask * (product(source, target, 1, 1) - observed)


def diagonal(square):
    row, col = grid_of(square.shape)
    return jnp.sum(jnp.where(row == col, square, 0.0), axis=0, keepdims=True)


def first_kernel(tiles, source_ref, target_ref, observed_ref, grad_ref, moving_ref, sums_ref):
    source, target = source_ref[...], target_ref[...]
    count = target.shape[0]
    residual = masked_residual(source, target, observed_ref[0], tiles[0, 0], tiles[0, 1])
    grad_source, grad_target = product(residual, target, 1, 0), product(residual, source, 0, 0)
    grad_ref[...] = grad_source
    moving_ref[:count, :] = target
    moving_ref[count:, :] = grad_target
    gram_source = product(source, source, 0, 0)
    gram_target = product(target, target, 0, 0)
    cross = product(source, grad_source, 0, 0)
    square_source = product(grad_source, grad_source, 0, 0)
    square_target = product(grad_target, grad_target, 0, 0)
    row, col = grid_of(cross.shape)
    upper = row <= col
    packed = (
        cross,
        jnp.where(upper, gram_source, gram_target),
        jnp.where(upper, square_source, square_target),
    )
    for place, square in enumerate(packed):
        for side in range(2):
            rows = slice(16 * place + 8 * side, 16 * place + 8 * side + 8)
            sums_ref[:, rows, :] = square[:, 128 * side : 128 * side + 128].reshape(PIECES, 8, 128)
    sums_ref[:, 48:56, :] = jnp.zeros((PIECES, 8, 128), jnp.float32)
    for place, square in enumerate((gram_target, square_target)):
        line = diagonal(square)
        for side in range(2):
            slot = 48 + 2 * place + side
            sums_ref[0, slot : slot + 1, :] = line[:, 128 * side : 128 * side + 128]


def unpacked(sums_ref, place):
    halves = [sums_ref[:, 16 * place + 8 * side : 16 * place + 8 * side + 8, :].reshape(256, 128) for side in range(2)]
    return jnp.concatenate(halves, 1)


def unpacked_pair(sums_ref, place):
    packed = unpacked(sums_ref, place)
    flipped = packed.T
    row, col = grid_of(packed.shape)
    line = jnp.concatenate([sums_ref[0, 46 + 2 * place + side : 47 + 2 * place + side, :] for side in range(2)], 1)
    first = jnp.where(row <= col, packed, flipped)
    second = jnp.where(row > col, packed, flipped)
    return first, jnp.where(row == col, line, second)


def updated_gram(gram, cross, square, inverse):
    moved = product(cross, inverse, 1, 0)
    twice = product(product(inverse, square, 1, 0), inverse, 1, 0)
    return gram - step_size * (moved + moved.T) + (step_size * step_size) * twice


def inverse_kernel(source_rows, target_rows, sums_ref, source_ref, grad_ref, gram_out, inverse_out, source_out):
    gram_out[0], gram_out[1] = unpacked_pair(sums_ref, 1)
    inverse_out[0] = gram_out[0] / source_rows
    inverse_out[1] = gram_out[1] / target_rows
    invert_pair(inverse_out)
    source_out[...] = source_ref[...] - step_size * product(grad_ref[...], inverse_out[1], 1, 0)


def target_step(moving_ref, inverse):
    count = moving_ref.shape[0] // 2
    return moving_ref[:count, :] - step_size * product(moving_ref[count:, :], inverse, 1, 0)


def second_kernel(tiles, inverse_ref, source_ref, moving_ref, observed_ref, target_out, residual_out, grad_out):
    target = target_step(moving_ref, inverse_ref[0])
    residual = masked_residual(source_ref[...], target, observed_ref[1], tiles[1, 0], tiles[1, 1])
    grad_out[...] = product(residual, source_ref[...], 0, 0)
    target_out[...] = target
    residual_out[...] = residual


def invert_pair_from(gram_ref, guess_ref, inverse_ref, error_ref):
    size = gram_ref.shape[1]
    row, col = grid_of((size, size))

    def residual():
        total = 0.0
        for t in range(2):
            error = jnp.where(row == col, 1.0, 0.0) - product(gram_ref[t], inverse_ref[t], 1, 0)
            error_ref[t] = error
            total += jnp.sum(error * error)
        return total

    def refine():
        for t in range(2):
            error = error_ref[t]
            error += product(error, error, 1, 0, lax.Precision.DEFAULT)
            inverse_ref[t] += product(inverse_ref[t], error, 1, 0)

    def turn(state):
        refine()
        return state[0] + 1, residual()

    inverse_ref[...] = guess_ref[...]
    _, total = lax.while_loop(
        lambda state: (state[0] < TURNS) & (state[1] > RESIDUAL * RESIDUAL), turn, (0, residual())
    )
    settled = total <= RESIDUAL * RESIDUAL

    @pl.when(settled)
    def _():
        refine()

    @pl.when(jnp.logical_not(settled))
    def _():
        inverse_ref[...] = gram_ref[...]
        invert_pair(inverse_ref)


def third_kernel(
    source_rows, target_rows,
    sums_ref, gram_ref, inverse_ref, source_ref, target_ref, residual_ref, leaving_ref,
    source_out, tail_out, moved, work, error,
):
    square_source, square_target = unpacked_pair(sums_ref, 2)
    cross = unpacked(sums_ref, 0)
    moved[0] = updated_gram(gram_ref[0], cross, square_source, inverse_ref[1]) / source_rows
    moved[1] = updated_gram(gram_ref[1], cross.T, square_target, inverse_ref[0]) / target_rows
    invert_pair_from(moved, inverse_ref, work, error)
    grad = product(residual_ref[...], target_ref[...], 1, 0)
    source_out[...] = source_ref[...] - step_size * product(grad, work[1], 1, 0)
    count = target_ref.shape[0]
    tail_out[:count, :] = target_step(leaving_ref, inverse_ref[0])
    tail_out[count:, :] = -step_size * work[0]


def call(kernel, shapes, scratch, *arguments, scalars=0):
    vmem = pl.BlockSpec(memory_space=pltpu.VMEM)
    smem = pl.BlockSpec(memory_space=pltpu.SMEM)
    return pl.pallas_call(
        kernel,
        out_shape=[jax.ShapeDtypeStruct(shape, jnp.float32) for shape in shapes],
        in_specs=[smem] * scalars + [vmem] * (len(arguments) - scalars),
        out_specs=[vmem] * len(shapes),
        scratch_shapes=[pltpu.VMEM(shape, jnp.float32) for shape in scratch],
    )(*arguments)


def moved_on(value, steps):
    count = lax.axis_size(WIDE)
    return lax.ppermute(value, WIDE, [(place, (place + steps) % count) for place in range(count)])


def exchanged(value, axes):
    return lax.all_to_all(value, axes, 0, 0, tiled=True)


def spread(value, axes):
    return exchanged(jnp.broadcast_to(value[None], (lax.axis_size(axes), *value.shape)), axes)


def on_device(source, target, observed, tiles):
    devices = lax.axis_size(AXES)
    source_rows = source.shape[0] * devices
    target_rows = target.shape[0] * devices
    flags = tiles.reshape(2, 2)
    square = (256, 256)
    grad, moving, sums = call(
        first_kernel, (square, square, (PIECES, 56, 128)), (), flags, source, target, observed, scalars=1
    )
    shape = sums.shape
    sums = jnp.sum(exchanged(sums.reshape(2, -1, 128), "core"), axis=0)
    sums = jnp.sum(exchanged(sums.reshape(-1, *shape[1:]), NEAR), axis=0)
    for axes in FAR:
        sums = jnp.sum(spread(sums, axes), axis=0)
    sums = spread(sums, NEAR).reshape(-1, 128)
    sums, moving = lax.optimization_barrier((spread(sums, "core").reshape(shape), moving))
    leaving = moved_on(moving, 2)
    moving = moved_on(moving, 1)

    def inverses(*refs):
        inverse_kernel(source_rows, target_rows, *refs)

    def final(*refs):
        third_kernel(source_rows, target_rows, *refs)

    pair = (2, *square)
    grams, inverse, source = call(inverses, (pair, pair, square), (), sums, source, grad)
    block = target.shape
    target, residual, grad = call(
        second_kernel, (block, (block[1], block[0]), block), (), flags, inverse, source, moving, observed, scalars=1
    )
    grad = moved_on(grad, 1)
    count = block[0]
    source, tail = call(
        final, (square, (count + 256, 256)), (pair, pair, pair), sums, grams, inverse, source, target, residual, leaving
    )
    return source, tail[:count] + product(grad, tail[count:], 1, 0)


def solution(mesh):
    fine = Mesh(mesh.devices.reshape((2,) * len(AXES)), AXES)
    placed = (P(AXES, None), P(AXES, None), P(None, AXES, None), P(None, AXES, None))
    return jax.shard_map(
        on_device, mesh=fine, in_specs=placed, out_specs=(P(AXES, None), P(AXES, None)), check_vma=False
    )
```

```python
import jax
import jax.numpy as jnp
from jax import lax
from jax.experimental import pallas as pl
from jax.experimental.pallas import tpu as pltpu
from jax.sharding import Mesh
from jax.sharding import PartitionSpec as P

step_size = 0.0002

AXES = ("xh", "xl", "ya", "yb", "yc", "zh", "zla", "zlb", "core")
WIDE = ("xh", "xl", "ya", "yb", "yc", "zh")
NEAR = ("xh", "xl", "yc", "zlb")
FAR = (("ya", "yb"), ("zh", "zla"))
PIECES = 32
BLOCK = 32
TURNS = 4
RESIDUAL = 0.003


def product(left, right, left_dim, right_dim, precision=lax.Precision.HIGHEST):
    return lax.dot_general(
        left,
        right,
        (((left_dim,), (right_dim,)), ((), ())),
        precision=precision,
        preferred_element_type=jnp.float32,
    )


def halves(value):
    high = value.astype(jnp.bfloat16)
    return high, (value - high.astype(jnp.float32)).astype(jnp.bfloat16)


def update_product(left, right, left_dim, right_dim):
    (left, left_low), (right, right_low) = halves(left), halves(right)
    dims = (left_dim, right_dim, lax.Precision.DEFAULT)
    small = product(left, right_low, *dims) + product(left_low, right, *dims)
    return product(left, right, *dims) + small


def grid_of(shape):
    return lax.broadcasted_iota(jnp.int32, shape, 0), lax.broadcasted_iota(jnp.int32, shape, 1)


def sweep_pair(panels, first):
    rows, cols = panels[0].shape
    sub, lane = grid_of((8, cols))
    if first:
        panels = [pltpu.roll(panel, cols - first, 1) for panel in panels]
    start = tuple(tuple(panel[8 * g : 8 * g + 8] for g in range(rows // 8)) for panel in panels)

    def wide(value):
        return jnp.broadcast_to(value, (8, cols))

    def eight_pivots(_, carry):
        held = [list(groups) for groups in carry]
        for r in range(0, 8, 4):
            for t, groups in enumerate(held):
                columns = [[wide(group[:, r + q : r + q + 1]) for group in groups] for q in range(4)]
                for pair in (0, 2):
                    k = r + pair
                    here, after = lane == k, lane == k + 1
                    left, right = columns[pair], columns[pair + 1]
                    upper = jnp.where(after, 0.0, jnp.where(here, 1.0, wide(groups[0][k : k + 1])))
                    lower = jnp.where(here, 0.0, jnp.where(after, 1.0, wide(groups[0][k + 1 : k + 2])))
                    main = jnp.where(sub == k, left[0], right[0])
                    cross = wide(jnp.where(sub == k, right[0], left[0])[k : k + 1])
                    one, two = wide(main[k : k + 1]), wide(main[k + 1 : k + 2])
                    scale = 1.0 / (one * two - cross * cross)

                    def swept(values, inside, upper, lower):
                        upper, lower = scale * (two * upper - cross * lower), scale * (one * lower - cross * upper)
                        values = [
                            (value if inside is None else jnp.where(inside, 0.0, value)) - left[g] * upper - right[g] * lower
                            for g, value in enumerate(values)
                        ]
                        values[0] = jnp.where(sub == k, upper, jnp.where(sub == k + 1, lower, values[0]))
                        return values

                    if pair == 0:
                        for q in (2, 3):
                            rows_of = jnp.where(sub == k, columns[q][0], columns[q][0] + 0.0 * one)
                            columns[q] = swept(columns[q], None, wide(rows_of[k : k + 1]), wide(rows_of[k + 1 : k + 2]))
                    groups = swept(groups, here | after, upper, lower)
                held[t] = groups
        return tuple(tuple(pltpu.roll(group, cols - 8, 1) for group in groups[1:] + groups[:1]) for groups in held)

    swept = [jnp.concatenate(groups, 0) for groups in lax.fori_loop(0, rows // 8, eight_pivots, start)]
    back = (first + rows) % cols
    return [pltpu.roll(panel, back, 1) for panel in swept] if back else swept


def invert_blocks(squares):
    size = squares[0].shape[0]
    lane = lax.broadcasted_iota(jnp.int32, (BLOCK, size), 1)
    panels = [[square[start : start + BLOCK] for start in range(0, size, BLOCK)] for square in squares]
    for block in range(size // BLOCK):
        start = block * BLOCK
        swept = sweep_pair([held[block] for held in panels], start)
        inside = (lane >= start) & (lane < start + BLOCK)
        for held, panel in zip(panels, swept):
            for other in range(len(held)):
                left = held[other][:, start : start + BLOCK]
                if other != block:
                    held[other] = jnp.where(inside, 0.0, held[other]) - product(left, panel, 1, 0)
            held[block] = panel
    return [jnp.concatenate(held, 0) for held in panels]


def invert_pair(ref):
    size = ref.shape[1]
    half = size // 2
    row, col = grid_of((size, size))
    scales = []
    for t in range(2):
        whole = ref[t]
        main = jnp.where(row == col, whole, 0.0)
        across = lax.rsqrt(jnp.sum(main, axis=0, keepdims=True))
        down = lax.rsqrt(jnp.sum(main, axis=1, keepdims=True))
        scales.append((across, down))
        ref[t] = whole * across * down
    leading = invert_blocks([ref[t, :half, :half] for t in range(2)])
    ratio = [product(leading[t], ref[t, :half, half:], 1, 0) for t in range(2)]
    rest = [ref[t, half:, half:] - product(ref[t, :half, half:], ratio[t], 0, 0) for t in range(2)]
    for t in range(2):
        ref[t, :half, :half] = leading[t]
        ref[t, :half, half:] = ratio[t]
    trailing = invert_blocks(rest)
    for t in range(2):
        across, down = scales[t]
        ratio = ref[t, :half, half:]
        corner = -product(ratio, trailing[t], 1, 0)
        top = ref[t, :half, :half] - product(corner, ratio, 1, 1)
        ref[t, :half, :half] = top * across[:, :half] * down[:half]
        ref[t, :half, half:] = corner * across[:, half:] * down[:half]
        ref[t, half:, :half] = corner.T * across[:, :half] * down[half:]
        ref[t, half:, half:] = trailing[t] * across[:, half:] * down[half:]


def masked_residual(source, target, observed, upper, lower):
    row = lax.broadcasted_iota(jnp.int32, observed.shape, 0)
    mask = jnp.where(row < observed.shape[0] // 2, upper, lower).astype(jnp.float32)
    return mask * (update_product(source, target, 1, 1) - observed)


def diagonal(square):
    row, col = grid_of(square.shape)
    return jnp.sum(jnp.where(row == col, square, 0.0), axis=0, keepdims=True)


def first_kernel(tiles, source_ref, target_ref, observed_ref, grad_ref, moving_ref, sums_ref):
    source, target = source_ref[...], target_ref[...]
    count = target.shape[0]
    residual = masked_residual(source, target, observed_ref[0], tiles[0, 0], tiles[0, 1])
    grad_source, grad_target = update_product(residual, target, 1, 0), update_product(residual, source, 0, 0)
    grad_ref[...] = grad_source
    moving_ref[:count, :] = target
    moving_ref[count:, :] = grad_target
    gram_source = product(source, source, 0, 0)
    gram_target = product(target, target, 0, 0)
    cross = update_product(source, grad_source, 0, 0)
    square_source = update_product(grad_source, grad_source, 0, 0)
    square_target = update_product(grad_target, grad_target, 0, 0)
    row, col = grid_of(cross.shape)
    upper = row <= col
    packed = (
        cross,
        jnp.where(upper, gram_source, gram_target),
        jnp.where(upper, square_source, square_target),
    )
    for place, square in enumerate(packed):
        for side in range(2):
            rows = slice(16 * place + 8 * side, 16 * place + 8 * side + 8)
            sums_ref[:, rows, :] = square[:, 128 * side : 128 * side + 128].reshape(PIECES, 8, 128)
    sums_ref[:, 48:56, :] = jnp.zeros((PIECES, 8, 128), jnp.float32)
    for place, square in enumerate((gram_target, square_target)):
        line = diagonal(square)
        for side in range(2):
            slot = 48 + 2 * place + side
            sums_ref[0, slot : slot + 1, :] = line[:, 128 * side : 128 * side + 128]


def unpacked(sums_ref, place):
    halves = [sums_ref[:, 16 * place + 8 * side : 16 * place + 8 * side + 8, :].reshape(256, 128) for side in range(2)]
    return jnp.concatenate(halves, 1)


def unpacked_pair(sums_ref, place):
    packed = unpacked(sums_ref, place)
    flipped = packed.T
    row, col = grid_of(packed.shape)
    line = jnp.concatenate([sums_ref[0, 46 + 2 * place + side : 47 + 2 * place + side, :] for side in range(2)], 1)
    first = jnp.where(row <= col, packed, flipped)
    second = jnp.where(row > col, packed, flipped)
    return first, jnp.where(row == col, line, second)


def updated_gram(gram, cross, square, inverse):
    moved = update_product(cross, inverse, 1, 0)
    twice = update_product(update_product(inverse, square, 1, 0), inverse, 1, 0)
    return gram - step_size * (moved + moved.T) + (step_size * step_size) * twice


def inverse_kernel(source_rows, target_rows, sums_ref, source_ref, grad_ref, gram_out, inverse_out, source_out):
    gram_out[0], gram_out[1] = unpacked_pair(sums_ref, 1)
    inverse_out[0] = gram_out[0] / source_rows
    inverse_out[1] = gram_out[1] / target_rows
    invert_pair(inverse_out)
    source_out[...] = source_ref[...] - step_size * update_product(grad_ref[...], inverse_out[1], 1, 0)


def target_step(moving_ref, inverse):
    count = moving_ref.shape[0] // 2
    return moving_ref[:count, :] - step_size * update_product(moving_ref[count:, :], inverse, 1, 0)


def second_kernel(tiles, inverse_ref, source_ref, moving_ref, observed_ref, target_out, residual_out, grad_out):
    target = target_step(moving_ref, inverse_ref[0])
    residual = masked_residual(source_ref[...], target, observed_ref[1], tiles[1, 0], tiles[1, 1])
    grad_out[...] = update_product(residual, source_ref[...], 0, 0)
    target_out[...] = target
    residual_out[...] = residual


def invert_pair_from(gram_ref, guess_ref, inverse_ref, error_ref):
    size = gram_ref.shape[1]
    row, col = grid_of((size, size))

    def residual():
        total = 0.0
        for t in range(2):
            error = jnp.where(row == col, 1.0, 0.0) - product(gram_ref[t], inverse_ref[t], 1, 0)
            error_ref[t] = error
            total += jnp.sum(error * error)
        return total

    def refine():
        for t in range(2):
            error = error_ref[t]
            error += product(error, error, 1, 0, lax.Precision.DEFAULT)
            inverse_ref[t] += product(inverse_ref[t], error, 1, 0)

    def turn(state):
        refine()
        return state[0] + 1, residual()

    inverse_ref[...] = guess_ref[...]
    _, total = lax.while_loop(
        lambda state: (state[0] < TURNS) & (state[1] > RESIDUAL * RESIDUAL), turn, (0, residual())
    )
    settled = total <= RESIDUAL * RESIDUAL

    @pl.when(settled)
    def _():
        refine()

    @pl.when(jnp.logical_not(settled))
    def _():
        inverse_ref[...] = gram_ref[...]
        invert_pair(inverse_ref)


def third_kernel(
    source_rows, target_rows,
    sums_ref, gram_ref, inverse_ref, source_ref, target_ref, residual_ref, leaving_ref,
    source_out, tail_out, moved, work, error,
):
    square_source, square_target = unpacked_pair(sums_ref, 2)
    cross = unpacked(sums_ref, 0)
    moved[0] = updated_gram(gram_ref[0], cross, square_source, inverse_ref[1]) / source_rows
    moved[1] = updated_gram(gram_ref[1], cross.T, square_target, inverse_ref[0]) / target_rows
    invert_pair_from(moved, inverse_ref, work, error)
    grad = update_product(residual_ref[...], target_ref[...], 1, 0)
    source_out[...] = source_ref[...] - step_size * update_product(grad, work[1], 1, 0)
    count = target_ref.shape[0]
    tail_out[:count, :] = target_step(leaving_ref, inverse_ref[0])
    tail_out[count:, :] = -step_size * work[0]


def call(kernel, shapes, scratch, *arguments, scalars=0):
    vmem = pl.BlockSpec(memory_space=pltpu.VMEM)
    smem = pl.BlockSpec(memory_space=pltpu.SMEM)
    return pl.pallas_call(
        kernel,
        out_shape=[jax.ShapeDtypeStruct(shape, jnp.float32) for shape in shapes],
        in_specs=[smem] * scalars + [vmem] * (len(arguments) - scalars),
        out_specs=[vmem] * len(shapes),
        scratch_shapes=[pltpu.VMEM(shape, jnp.float32) for shape in scratch],
    )(*arguments)


def moved_on(value, steps):
    count = lax.axis_size(WIDE)
    return lax.ppermute(value, WIDE, [(place, (place + steps) % count) for place in range(count)])


def exchanged(value, axes):
    return lax.all_to_all(value, axes, 0, 0, tiled=True)


def spread(value, axes):
    return exchanged(jnp.broadcast_to(value[None], (lax.axis_size(axes), *value.shape)), axes)


def on_device(source, target, observed, tiles):
    devices = lax.axis_size(AXES)
    source_rows = source.shape[0] * devices
    target_rows = target.shape[0] * devices
    flags = tiles.reshape(2, 2)
    square = (256, 256)
    grad, moving, sums = call(
        first_kernel, (square, square, (PIECES, 56, 128)), (), flags, source, target, observed, scalars=1
    )
    shape = sums.shape
    sums = jnp.sum(exchanged(sums.reshape(2, -1, 128), "core"), axis=0)
    sums = jnp.sum(exchanged(sums.reshape(-1, *shape[1:]), NEAR), axis=0)
    for axes in FAR:
        sums = jnp.sum(spread(sums, axes), axis=0)
    sums = spread(sums, NEAR).reshape(-1, 128)
    sums, moving = lax.optimization_barrier((spread(sums, "core").reshape(shape), moving))
    leaving = moved_on(moving, 2)
    moving = moved_on(moving, 1)

    def inverses(*refs):
        inverse_kernel(source_rows, target_rows, *refs)

    def final(*refs):
        third_kernel(source_rows, target_rows, *refs)

    pair = (2, *square)
    grams, inverse, source = call(inverses, (pair, pair, square), (), sums, source, grad)
    block = target.shape
    target, residual, grad = call(
        second_kernel, (block, (block[1], block[0]), block), (), flags, inverse, source, moving, observed, scalars=1
    )
    grad = moved_on(grad, 1)
    count = block[0]
    source, tail = call(
        final, (square, (count + 256, 256)), (pair, pair, pair), sums, grams, inverse, source, target, residual, leaving
    )
    return source, tail[:count] + product(grad, tail[count:], 1, 0)


def solution(mesh):
    fine = Mesh(mesh.devices.reshape((2,) * len(AXES)), AXES)
    placed = (P(AXES, None), P(AXES, None), P(None, AXES, None), P(None, AXES, None))
    return jax.shard_map(
        on_device, mesh=fine, in_specs=placed, out_specs=(P(AXES, None), P(AXES, None)), check_vma=False
    )
```
